32 devices in a mesh: clus: 4 (over y, x), trip: 4 (over z), mode: 2 (over core).
Axes of the slice: x: 2, y: 2, z: 4, core: 2. Of those that a mesh axis runs over, the one named last changes fastest.
Arguments:
- force_third: bfloat16 [8, 90, 8100], P('clus', 'mode'), may hold values from -0.0234375 to 0.0234375
- phase_angle: bfloat16 [8, 16], P('clus', 'trip'), may hold values from -3.140625 to 3.140625
- eigenvectors: bfloat16 [32, 90, 180], P('trip'), may hold values from -0.4375 to 0.4375
- frequencies: bfloat16 [32, 90], P('trip'), may hold values from 0.5 to 2
- deviation: bfloat16 [32, 90], P('trip'), may hold values from 0.5 to 2
- send_rows: int32 [4, 32], P('trip'), may hold values from 0 to 7
- trip_table: int32 [16, 3], P('trip'), may hold values from 0 to 31
- irreducible: int32 [16], P('trip'), may hold values from 0 to 3
- multiplicity: int32 [16], P('trip'), may hold values from 1 to 8
- drive_term: float32 [4, 90], P('trip', 'mode'), may hold values from -120 to 120
- boundary: float32 [4, 90], P('trip', 'mode'), may hold values from 5 to 40
Outputs:
- gamma_total: float32 [4, 90], P('trip', 'mode')
- new_deviation: float32 [4, 90], P('trip', 'mode')
The draws below stay inside these ranges and needn't reach their ends.
All inputs are finite; a program needn't handle non-finite values.
Results may differ from the reference program's by a relative error of at most 0.00095.
Values may be sent and summed in bfloat16 or wider, within the bound.
A program may use at most 64 MiB of HBM per device.

```python
import math
import jax
import jax.numpy as jnp
from jax import lax

M = 90
CL_DEV = 2
G_DEV = 8
RECV = 32
NR = 8
TT = 4
TRIPLETS = 16
NG = 32
NQ = 4
SLOT = 8
N_CLUS = 4
N_TRIP = 4


def with_ends(values, rng, smallest, top_value):
    dims = values.shape
    index_at = [jax.random.randint(jax.random.fold_in(rng, axis), (), 0, dims[axis]) for axis in range(len(dims))]
    values = values.at[tuple(index_at)].set(smallest)
    longest = dims.index(max(dims))
    index_at[longest] = (index_at[longest] + 1) % dims[longest]
    return values.at[tuple(index_at)].set(top_value)


def levels(own_key, extent, pieces, least, largest):
    def one(position, blocks):
        draws = jax.random.uniform(jax.random.fold_in(jax.random.fold_in(own_key, 6), position), (blocks,), jnp.float32, least / len(pieces), largest / len(pieces))
        return jnp.repeat(jnp.exp(draws), extent[position] // blocks).reshape((-1,) + (1,) * (len(extent) - position - 1))

    factor_of = one(*pieces[0])
    for cut in pieces[1:]:
        factor_of = factor_of * one(*cut)
    return factor_of


def bell_draw(key, extent, scale, bound, cuts=(), kind=jnp.bfloat16):
    result = jax.random.normal(key, extent, jnp.float32) * scale
    if len(cuts) > 0:
        result = levels(key, extent, cuts, -0.22, 0.18) * result
    return jnp.clip(result, min=-bound, max=bound).astype(kind)


def setup_inputs(seed: int = 0) -> dict:
    seeds = jax.random.split(jax.random.key(seed), 12)
    force_third = bell_draw(seeds[0], (NR, M, M * M), (M * M * NR) ** -0.5, 0.0234375, ((0, 4), (1, 2)))
    phase_angle = jnp.clip(jax.random.uniform(seeds[1], (NR, TRIPLETS), jnp.float32, -3.140625, 3.140625), -3.140625, 3.140625).astype(jnp.bfloat16)
    eigenvectors = bell_draw(seeds[2], (NG, M, 2 * M), (2 * M) ** -0.5, 0.4375, ((0, 4),))
    frequencies = jnp.clip(jnp.exp(math.log(2.0) - 1.3862944 * jax.random.uniform(seeds[3], (NG, M), jnp.float32) ** levels(seeds[3], (NG, M), ((0, 4),), -0.2, 0.2)), 0.5, 2.0).astype(jnp.bfloat16)
    deviation = jnp.clip(0.5 + 1.5 * jax.random.uniform(seeds[4], (NG, M), jnp.float32) ** levels(seeds[4], (NG, M), ((0, 4),), -0.2, 0.2), 0.5, 2.0).astype(jnp.bfloat16)
    send_rows = with_ends(jax.random.randint(seeds[5], (N_TRIP, RECV), 0, G_DEV), jax.random.fold_in(seeds[5], 1), 0, G_DEV - 1).astype(jnp.int32)
    trip_table = with_ends(jax.random.randint(seeds[6], (TRIPLETS, 3), 0, RECV), jax.random.fold_in(seeds[6], 1), 0, RECV - 1).astype(jnp.int32)
    irreducible = with_ends(jax.random.randint(seeds[7], (TRIPLETS,), 0, NQ), jax.random.fold_in(seeds[7], 1), 0, NQ - 1).astype(jnp.int32)
    multiplicity = with_ends(jax.random.randint(seeds[8], (TRIPLETS,), 1, 9), jax.random.fold_in(seeds[8], 1), 1, 8).astype(jnp.int32)
    drive_term = bell_draw(seeds[9], (NQ, M), 20.0, 120.0, ((0, 4), (1, 2)), jnp.float32)
    boundary = jnp.clip(jnp.exp(math.log(40.0) - 2.0794415 * jax.random.uniform(seeds[10], (NQ, M), jnp.float32) ** levels(seeds[10], (NQ, M), ((0, 4), (1, 2)), -0.2, 0.2)), 5.0, 40.0)
    return dict(force_third=force_third, phase_angle=phase_angle, eigenvectors=eigenvectors, frequencies=frequencies, deviation=deviation, send_rows=send_rows, trip_table=trip_table, irreducible=irreducible, multiplicity=multiplicity, drive_term=drive_term, boundary=boundary)


smearing = 0.3
highest = lax.Precision.HIGHEST


def rounded(values):
    return lax.optimization_barrier(values.astype(jnp.bfloat16)).astype(jnp.float32)


def gaussian_weights(freq_zero, freq_one, freq_two):
    decays = freq_zero - freq_one - freq_two
    merges = freq_zero + freq_one - freq_two
    scaled = 0.5 / (smearing * smearing)
    return (jnp.exp(-scaled * decays * decays) + jnp.exp(-scaled * merges * merges)) / (freq_zero * freq_one * freq_two)


def combine(by_real, by_imag, mode_count):
    return jnp.concatenate([by_real[..., :mode_count] - by_imag[..., mode_count:], by_real[..., mode_count:] + by_imag[..., :mode_count]], axis=-1)


def interaction(transform, vectors):
    mode_count = vectors.shape[1]
    real_part = transform[0].reshape(-1, mode_count)
    imag_part = transform[1].reshape(-1, mode_count)
    last_vec = vectors[2]
    flipped = jnp.concatenate([-last_vec[:, mode_count:], last_vec[:, :mode_count]], axis=1)
    section_one = jnp.dot(real_part, last_vec, precision=highest) + jnp.dot(imag_part, flipped, precision=highest)
    section_one = rounded(section_one).reshape(mode_count, mode_count, 2 * mode_count)
    middle = vectors[1]
    section_two = rounded(combine(jnp.einsum("abk,bj->ajk", section_one, middle[:, :mode_count], precision=highest), jnp.einsum("abk,bj->ajk", section_one, middle[:, mode_count:], precision=highest), mode_count))
    leading = vectors[0]
    return combine(jnp.einsum("as,ajk->sjk", leading[:, :mode_count], section_two, precision=highest), jnp.einsum("as,ajk->sjk", leading[:, mode_count:], section_two, precision=highest), mode_count)


def reference(force_third, phase_angle, eigenvectors, frequencies, deviation, send_rows, trip_table, irreducible, multiplicity, drive_term, boundary):
    clusters = force_third.astype(jnp.float32).reshape(N_CLUS, CL_DEV, M * M * M)
    triplets = jnp.arange(TRIPLETS, dtype=jnp.int32)
    owners = triplets // TT
    sources = trip_table // SLOT
    within = trip_table % SLOT
    grid_points = sources * G_DEV + send_rows[sources, owners[:, None] * SLOT + within]
    vectors_all = eigenvectors.astype(jnp.float32)
    freq_all = frequencies.astype(jnp.float32)
    occupied_all = deviation.astype(jnp.float32)

    def one_triplet(triplet):
        angles = phase_angle[:, triplet].astype(jnp.float32).reshape(N_CLUS, CL_DEV)
        cosines = rounded(jnp.cos(angles))
        sines = rounded(jnp.sin(angles))
        real_sum = rounded(jnp.sum(rounded(jnp.einsum("gr,grx->gx", cosines, clusters, precision=highest)), axis=0))
        imag_sum = rounded(jnp.sum(rounded(jnp.einsum("gr,grx->gx", sines, clusters, precision=highest)), axis=0))
        transform = jnp.stack([real_sum, imag_sum]).reshape(2, M, M * M)
        members = grid_points[triplet]
        amplitude = interaction(transform, vectors_all[members])
        squared = amplitude[..., :M] ** 2 + amplitude[..., M:] ** 2
        rates = freq_all[members]
        weights = squared * gaussian_weights(rates[0][:, None, None], rates[1][None, :, None], rates[2][None, None, :]) * multiplicity[triplet].astype(jnp.float32)
        occupied = occupied_all[members]
        totals = jnp.sum(weights, axis=(1, 2))
        couples = jnp.einsum("sjk,j->s", weights, occupied[1], precision=highest) + jnp.einsum("sjk,k->s", weights, occupied[2], precision=highest)
        return totals, couples

    totals, couples = lax.map(one_triplet, triplets)
    onehot = (irreducible[:, None] == jnp.arange(NQ, dtype=jnp.int32)[None, :]).astype(jnp.float32)
    rate = jnp.dot(onehot.T, totals, precision=highest)
    coupled = jnp.dot(onehot.T, couples, precision=highest)
    gamma_total = rate + boundary
    return gamma_total, (drive_term + coupled) / gamma_total
```

```python
import functools

import jax
import jax.numpy as jnp
from jax import lax
from jax.experimental import pallas as pl
from jax.experimental.pallas import tpu as pltpu
from jax.sharding import PartitionSpec as P

smearing = 0.3
MESH = pl.DeviceIdType.MESH
LANES = 128
SUB = 16
WORKERS = 8
f32 = jnp.float32
bf16 = jnp.bfloat16


def up(value, step):
    return -(-value // step) * step


def pick(index, options):
    chosen = options[0]
    for position in range(1, len(options)):
        chosen = jnp.where(index == position, options[position], chosen)
    return chosen


def flip(bit, by):
    return bit + by - 2 * bit * by


def plan(flat):
    left = -(-flat // (WORKERS * LANES))
    units = [1] if left > 2 else []
    left -= sum(units)
    while left > 0:
        units.append(min(2, left))
        left -= units[-1]
    rounds, base, col = [], 0, 0
    for index, unit in enumerate(units):
        rounds.append((index % 2, base, unit * LANES, col))
        base += unit * LANES * WORKERS
        col += unit * LANES
    return rounds


def kernel(
    dims,
    force_ref,
    angle_ref,
    eig_ref,
    freq_ref,
    occ_ref,
    send_rows_ref,
    table_ref,
    irr_ref,
    mult_ref,
    drive_ref,
    bound_ref,
    gamma_ref,
    dev_ref,
    own,
    fbuf,
    gout,
    gin,
    gsib,
    tails,
    lset,
    wphase,
    wz,
    left,
    ehalf,
    asked,
    wanted,
    outgoing,
    arrived,
    mine,
    other,
    ebuf,
    zbuf,
    tre,
    tim,
    w0buf,
    gauss,
    ratebuf,
    coupbuf,
    msg,
    inbox,
    f_send,
    f_recv,
    g_send,
    g_recv,
    s_send,
    s_recv,
    t_send,
    t_recv,
    c_send,
    c_recv,
    e_send,
    e_recv,
    p_send,
    p_recv,
    m_send,
    m_recv,
):
    n_clus, n_trip, n_mode, modes, half, rp, cl, slot, rounds = dims
    ep = up(modes + 1, 16)
    flat = force_ref.shape[2]
    wide = own.shape[1]
    c = lax.axis_index("clus")
    t = lax.axis_index("trip")
    m = lax.axis_index("mode")
    k = lax.rem(t, 2)
    tz = t + 1 - 2 * k
    bits = (lax.rem(c, 2), c // 2)
    step = (1 - 2 * bits[0], 2 - 4 * bits[1])
    sib = (c, t, 1 - m)
    first = m == 0

    peers = []
    for dt in range(n_trip):
        for dc in range(n_clus):
            if dt or dc:
                peers.append((dt, dc))

    def peer_id(dt, dc):
        return (lax.rem(c + dc, n_clus), lax.rem(t + dt, n_trip), m)

    def clus_at(axis, du):
        return c + step[axis] if du else c

    across = [sib]
    for axis in range(2):
        for dk in range(2):
            across.append((clus_at(axis, 1), tz if dk else t, 1 - m))
    across.append((c, tz, 1 - m))

    barrier = pltpu.get_barrier_semaphore()
    for dt, dc in peers:
        pl.semaphore_signal(barrier, inc=1, device_id=peer_id(dt, dc), device_id_type=MESH)
    for device in across:
        pl.semaphore_signal(barrier, inc=1, device_id=device, device_id_type=MESH)

    asked[...] = jnp.zeros_like(asked)
    for j in range(3):
        asked[j : j + 1, :] = jnp.full((1, LANES), table_ref[c, j].astype(f32))

    whole = half // 16 * 16
    edge = flat // LANES * LANES
    for r in range(cl):
        at = r * rp
        if edge < wide:
            own[at : at + rp, edge:wide] = jnp.zeros((rp, wide - edge), bf16)
        own[at : at + whole, :flat] = force_ref[r, :whole, :]
        rest = force_ref[r, whole:, :].astype(f32)
        under = jnp.zeros((rp - half, flat), f32)
        own[at + whole : at + rp, :flat] = jnp.concatenate([rest, under], axis=0).astype(bf16)

    angles = angle_ref[...].astype(f32)
    here = k * n_clus + c
    tails[here] = jnp.zeros((8, LANES), f32)
    tails[here, 0:cl, 0 : angles.shape[1]] = jnp.cos(angles).astype(bf16).astype(f32)
    tails[here, cl : 2 * cl, 0 : angles.shape[1]] = jnp.sin(angles).astype(bf16).astype(f32)

    points = eig_ref.shape[0]
    ehalf[...] = jnp.zeros_like(ehalf)
    for p in range(points):
        both = eig_ref[p].astype(f32)
        ehalf[p, 0:half, 0 : 2 * modes] = pick(m, [both[h * half : (h + 1) * half] for h in range(n_mode)])
    extra = jnp.where(first, freq_ref[...].astype(f32), occ_ref[...].astype(f32))
    for p in range(points):
        ehalf[p, half : half + 1, 0:modes] = extra[p : p + 1]

    pl.semaphore_wait(barrier, len(peers) + len(across))

    started = []

    def remote(src, dst, send_sem, recv_sem, device):
        return pltpu.make_async_remote_copy(
            src_ref=src,
            dst_ref=dst,
            send_sem=send_sem,
            recv_sem=recv_sem,
            device_id=device,
            device_id_type=MESH,
        )

    def send(src, dst, send_sem, recv_sem, device):
        copy = remote(src, dst, send_sem, recv_sem, device)
        copy.start()
        started.append(copy)

    asks = []
    for dt in range(1, n_trip):
        copy = remote(asked, wanted.at[dt], t_send.at[dt], t_recv.at[dt], (c, lax.rem(t + dt, n_trip), m))
        copy.start()
        asks.append(copy)

    cube = []
    cube_clus = [c, c + step[0], c + step[1], c + step[0] + step[1]]
    for dk in range(2):
        for dc in range(n_clus):
            if dk or dc:
                cube.append((dk, dc))
    for index, (dk, dc) in enumerate(cube):
        send(
            tails.at[here],
            tails.at[here],
            c_send.at[index],
            c_recv.at[here],
            (cube_clus[dc], tz if dk else t, m),
        )

    def worker(ub, kk, mm):
        return (ub * 2 + kk) * 2 + mm

    def columns(e, w):
        _, base, width, _ = rounds[e]
        return pl.ds(pl.multiple_of(base + w * width, LANES), width)

    def local(e):
        return pl.ds(rounds[e][3], rounds[e][2])

    def lines(e):
        axis = rounds[e][0]
        cu, cv = clus_at(axis, 1), clus_at(1 - axis, 1)
        return bits[axis], cu, cv, c + step[0] + step[1]

    def direct(e):
        ub, cu, cv, _ = lines(e)
        dst = fbuf.at[m, c, :, local(e)]
        recv = f_recv.at[e, m, c]
        for index, mm in enumerate((m, 1 - m)):
            send(own.at[:, columns(e, worker(1 - ub, k, mm))], dst, f_send.at[e, index], recv, (cu, t, mm))
            send(own.at[:, columns(e, worker(ub, k, mm))], dst, f_send.at[e, 2 + index], recv, (cv, t, mm))
        send(own.at[:, columns(e, worker(ub, k, 1 - m))], dst, f_send.at[e, 4], recv, sib)

    def got(e, g, cc):
        ref = fbuf.at[g, cc, :, local(e)]
        remote(ref, ref, f_send.at[e, 0], f_recv.at[e, g, cc], sib).wait_recv()

    def forward(e):
        _, cu, cv, _ = lines(e)
        for g in range(n_mode):
            got(e, g, cu)
            ref = fbuf.at[g, cu, :, local(e)]
            send(ref, ref, f_send.at[e, 5 + g], f_recv.at[e, g, cu], (cv, t, m))

    def phased(e):
        axis = rounds[e][0]
        ub, _, cv, cd = lines(e)
        me = worker(ub, k, m)
        fbuf[m, c, :, local(e)] = own[:, columns(e, me)]
        got(e, 1 - m, c)
        for g in range(n_mode):
            got(e, g, cv)
            got(e, g, cd)
        weights = wphase[axis]
        for g in range(n_mode):
            for a0 in range(0, rp, SUB):
                parts = []
                for cc in range(n_clus):
                    for r in range(cl):
                        parts.append(fbuf[g, cc, r * rp + a0 : r * rp + a0 + SUB, local(e)])
                out = jnp.dot(weights, jnp.concatenate(parts, axis=0), preferred_element_type=f32).astype(bf16)
                for q in range(4):
                    for i in range(2):
                        row = (q * 2 + i) * SUB
                        gout[q, g, i * rp + a0 : i * rp + a0 + SUB, local(e)] = out[row : row + SUB]
        dst = gin.at[:, columns(e, me)]
        recv = g_recv.at[e, me]
        index = 0
        for du, dk in ((1, 1), (0, 1), (1, 0)):
            for g in range(n_mode):
                device = (clus_at(axis, du), tz if dk else t, g)
                send(gout.at[du * 2 + dk, g, :, local(e)], dst, g_send.at[e, index], recv, device)
                index += 1
        send(gout.at[0, 1 - m, :, local(e)], dst, g_send.at[e, index], recv, sib)
        gin[:, columns(e, me)] = gout[0, m, :, local(e)]

    def gather(e):
        axis, base, width, _ = rounds[e]
        ub = bits[axis]
        for du in range(2):
            for dk in range(2):
                for dm in range(2):
                    if du or dk or dm:
                        w = worker(flip(ub, du), flip(k, dk), flip(m, dm))
                        ref = gin.at[:, columns(e, w)]
                        remote(ref, ref, g_send.at[e, 0], g_recv.at[e, w], sib).wait_recv()
        span = pl.ds(base, WORKERS * width)
        send(gin.at[:, span], gsib.at[:, span], s_send.at[e], s_recv.at[e], sib)

    def answer(dt, wishes):
        target = lax.rem(t - dt + n_trip, n_trip)
        for j in range(3):
            wish = wishes[j : j + 1, 0:1]
            block = jnp.zeros(ehalf.shape[1:], f32)
            for p in range(slot):
                row = send_rows_ref[0, target * slot + p]
                name = (t * slot + p).astype(f32)
                block = jnp.where(wish == name, ehalf[row], block)
            outgoing[dt, j] = block.astype(bf16)

    eig_copies = []

    def answers():
        for dt in range(1, n_trip):
            asks[dt - 1].wait()
            answer(dt, wanted[dt])
        for dt in range(1, n_trip):
            copy = remote(
                outgoing.at[dt],
                arrived.at[dt],
                e_send.at[dt],
                e_recv.at[dt],
                (c, lax.rem(t - dt + n_trip, n_trip), m),
            )
            copy.start()
            eig_copies.append(copy)
        answer(0, asked[...])
        arrived[0] = outgoing[0]

    lane = lax.broadcasted_iota(jnp.int32, (1, LANES), 1)

    def phase_weights():
        for dk, dc in cube:
            there = flip(k, dk) * n_clus + cube_clus[dc]
            ref = tails.at[there]
            remote(ref, ref, c_send.at[0], c_recv.at[there], sib).wait_recv()
        stack = jnp.concatenate([tails[i] for i in range(2 * n_clus)], axis=0)
        stack = jnp.concatenate([stack, jnp.zeros((LANES - stack.shape[0], LANES), f32)], axis=0)
        turned = jnp.transpose(stack)[:SUB].astype(bf16)
        row = lax.broadcasted_iota(jnp.int32, (LANES, LANES), 0)
        col = lax.broadcasted_iota(jnp.int32, (LANES, LANES), 1)
        source = (col // (cl * SUB)) * 8 + lax.rem(col // SUB, cl)
        for kk in range(2):
            for i in range(2):
                spread = jnp.where(row == source + (kk * n_clus * 8 + i * cl), 1.0, 0.0).astype(bf16)
                lset[kk * 2 + i] = jnp.dot(turned, spread, preferred_element_type=f32)
        same = lax.broadcasted_iota(jnp.int32, (SUB, LANES), 0) == lax.rem(
            lax.broadcasted_iota(jnp.int32, (SUB, LANES), 1), SUB
        )
        for axis in range(2):
            for du in range(2):
                for dk in range(2):
                    for i in range(2):
                        values = lset[flip(k, dk) * 2 + i, pl.ds(clus_at(axis, du), 1), :]
                        at = ((du * 2 + dk) * 2 + i) * SUB
                        wphase[axis, at : at + SUB, :] = jnp.where(same, values, 0.0).astype(bf16)

    pair = remote(mine, other, p_send, p_recv, sib)

    def members():
        for copy in eig_copies:
            copy.wait()
        for j in range(3):
            source = table_ref[c, j] // slot
            mine[j] = arrived[lax.rem(source - t + n_trip, n_trip), j]
        pair.start()

    fill = jnp.zeros((LANES - 2 * rp, LANES), f32)
    state = {}

    def half_rows(mat, which):
        return pick(which, [mat[h * half : h * half + rp] for h in range(n_mode)])

    def column(row):
        return jnp.transpose(jnp.broadcast_to(row, (LANES, LANES)))

    def vectors():
        pair.wait()
        ebuf[...] = jnp.zeros_like(ebuf)
        freqs, occs = [], []
        for j in range(3):
            a = mine[j].astype(f32)
            b = other[j].astype(f32)
            parts = jnp.where(first, a, b), jnp.where(first, b, a)
            for g in range(n_mode):
                at = g * rp if j == 0 else g * half
                ebuf[j, 0, at : at + half, 0:modes] = parts[g][:half, 0:modes]
                ebuf[j, 1, at : at + half, 0:modes] = parts[g][:half, modes : 2 * modes]
            w0buf[2 * j : 2 * j + 1, 0:LANES] = parts[0][half : half + 1, 0:LANES]
            w0buf[2 * j + 1 : 2 * j + 2, 0:LANES] = parts[1][half : half + 1, 0:LANES]
            freqs.append(w0buf[2 * j : 2 * j + 1, :])
            occs.append(w0buf[2 * j + 1 : 2 * j + 2, :])
        f0, f1, f2 = freqs
        _, d1, d2 = occs
        for place, g in enumerate((m, 1 - m)):
            re0 = ebuf[0, 0, pl.ds(pl.multiple_of(g * rp, 16), rp), :]
            im0 = ebuf[0, 1, pl.ds(pl.multiple_of(g * rp, 16), rp), :]
            real = half_rows(jnp.transpose(jnp.concatenate([re0, -im0, fill], axis=0)), m)
            imag = half_rows(jnp.transpose(jnp.concatenate([im0, re0, fill], axis=0)), m)
            turned = jnp.concatenate([real, imag], axis=0)[:, : 2 * rp].astype(bf16)
            wz[:, place * 2 * rp : (place + 1) * 2 * rp] = turned
        re1, im1 = ebuf[1, 0], ebuf[1, 1]
        re2, im2 = ebuf[2, 0], ebuf[2, 1]
        state["e2a"] = jnp.concatenate([re2, im2], axis=1)[:modes].astype(bf16)
        state["e2b"] = jnp.concatenate([-im2, re2], axis=1)[:modes].astype(bf16)
        tall = jnp.zeros((LANES - ep, LANES), f32)
        e1re_t = jnp.transpose(jnp.concatenate([re1, tall], axis=0))[:ep, :ep]
        e1im_t = jnp.transpose(jnp.concatenate([im1, tall], axis=0))[:ep, :ep]
        left[:, :ep] = jnp.concatenate([e1re_t, e1im_t], axis=0).astype(bf16)
        left[:, ep:] = jnp.concatenate([-e1im_t, e1re_t], axis=0).astype(bf16)
        row_id = lax.broadcasted_iota(jnp.int32, (ep, LANES), 0)
        state["w0row"] = f0
        state["w0"] = half_rows(column(f0), m)
        w1 = jnp.where(row_id < modes, column(f1)[:ep], 1.0)
        w2 = jnp.where(lane < modes, f2, 1.0)
        state["occ"] = jnp.where(row_id < modes, column(d1)[:ep], 0.0) + jnp.where(lane < modes, d2, 0.0)
        state["inverse"] = 1.0 / (w1 * w2)
        state["lower"] = w1 + w2
        state["upper"] = w1 - w2
        tre[modes * rp :, :] = jnp.zeros(((ep - modes) * rp, LANES), f32)
        tim[modes * rp :, :] = jnp.zeros(((ep - modes) * rp, LANES), f32)
        w0buf[8:, :] = state["w0"]

    scaled = 0.5 / (smearing * smearing)

    def gaussians(lo, hi):
        lower, upper, inverse = state["lower"], state["upper"], state["inverse"]

        def one(s, carry):
            w0 = w0buf[pl.ds(8 + s, 1), :]
            decays = w0 - lower
            merges = w0 + upper
            both = jnp.exp(-scaled * (decays * decays)) + jnp.exp(-scaled * (merges * merges))
            gauss[s] = both * inverse
            return carry

        lax.fori_loop(lo, hi, one, 0)

    def contract(e):
        _, base, width, _ = rounds[e]
        lo, hi = base, base + WORKERS * width
        span = pl.ds(lo, hi - lo)
        ref = gsib.at[:, span]
        remote(ref, ref, s_send.at[e], s_recv.at[e], sib).wait_recv()
        for at in range(lo, hi, 512):
            cols = slice(at, at + 512)
            both = jnp.concatenate([gin[:, cols], gsib[:, cols]], axis=0)
            zbuf[:, cols] = jnp.dot(wz[...], both, preferred_element_type=f32)
        for b in range(modes):
            if not lo < (b + 1) * modes <= hi:
                continue
            part = zbuf[:, b * modes : (b + 1) * modes].astype(bf16)
            out = jnp.dot(part[:rp], state["e2a"], preferred_element_type=f32) + jnp.dot(
                part[rp:], state["e2b"], preferred_element_type=f32
            )
            tre[b * rp : (b + 1) * rp, :] = out[:, :LANES]
            tim[b * rp : (b + 1) * rp, :] = out[:, LANES:]

    total = len(rounds)

    direct(0)
    if total > 1:
        direct(1)
    forward(0)
    if total > 2:
        direct(2)
    answers()
    phase_weights()
    for e in range(total):
        if e + 1 < total:
            forward(e + 1)
        if e + 3 < total:
            direct(e + 3)
        phased(e)
        if e == 1:
            members()
        if e == 2:
            gather(0)
            vectors()
        if e >= 3:
            gather(e - 2)
            contract(e - 3)
            gaussians((e - 3) * rp // 2, (e - 2) * rp // 2)
    gaussians(max(total - 3, 0) * rp // 2, rp)
    for e in range(max(total - 3, 0), total):
        if e + 1 < total:
            gather(e + 1)
        contract(e)

    occ = state["occ"]

    def one_pair(s0):
        def rows(ref):
            return jnp.concatenate(
                [ref[pl.ds(s0 + i, ep, stride=rp), :] for i in range(2)], axis=1
            ).astype(bf16)

        both = jnp.concatenate([rows(tre), rows(tim)], axis=0)
        amp = jnp.dot(left[...], both, preferred_element_type=f32)
        square = amp * amp
        square = square[:ep] + square[ep:]
        for i in range(2):
            value = square[:, i * LANES : (i + 1) * LANES] * gauss[s0 + i]
            at = pl.ds(pl.multiple_of((s0 + i) * 8, 8), 8)
            ratebuf[at, :] = jnp.sum(value.reshape(ep // 8, 8, LANES), axis=0)
            coupbuf[at, :] = jnp.sum((value * occ).reshape(ep // 8, 8, LANES), axis=0)

    group = 4

    def modes_step(p, carry):
        for i in range(group):
            one_pair((p * group + i) * 2)
        return carry

    lax.fori_loop(0, rp // (2 * group), modes_step, 0)

    def folded(ref):
        total = ref[pl.ds(0, rp, stride=8), :]
        for i in range(1, 8):
            total = total + ref[pl.ds(i, rp, stride=8), :]
        return jnp.sum(jnp.transpose(total), axis=0, keepdims=True)[:, :half]

    factor = mult_ref[c].astype(f32)
    f0 = state["w0row"]
    w0_row = pick(m, [f0[:, h * half : (h + 1) * half] for h in range(n_mode)])
    rate = folded(ratebuf) / w0_row * factor
    coup = folded(coupbuf) / w0_row * factor
    msg[...] = jnp.zeros_like(msg)
    msg[0:1, 0:half] = rate
    msg[1:2, 0:half] = coup
    msg[2:3, :] = jnp.full((1, LANES), irr_ref[c].astype(f32))

    copies = []
    for index, (dt, dc) in enumerate(peers):
        copy = remote(msg, inbox.at[index], m_send.at[index], m_recv.at[index], peer_id(dt, dc))
        copy.start()
        copies.append(copy)
    for copy in started:
        copy.wait_send()
    for copy in copies:
        copy.wait()

    nq = gamma_ref.shape[0]
    for q in range(nq):
        name = (t * nq + q).astype(f32)

        def kept(tile):
            return jnp.where(tile[2:3, :half] == name, tile[0:2, :half], 0.0)

        total = kept(msg[...])
        if len(peers) <= 16:
            for index in range(len(peers)):
                total = total + kept(inbox[index])
        else:
            total = lax.fori_loop(0, len(peers), lambda i, acc: acc + kept(inbox[i]), total)
        gamma = total[0:1] + bound_ref[q : q + 1, :]
        gamma_ref[q : q + 1, :] = gamma
        dev_ref[q : q + 1, :] = (drive_ref[q : q + 1, :] + total[1:2]) / gamma


def body(
    force_third,
    phase_angle,
    eigenvectors,
    frequencies,
    deviation,
    send_rows,
    trip_table,
    irreducible,
    multiplicity,
    drive_term,
    boundary,
):
    n_clus, n_trip, n_mode = (lax.axis_size(name) for name in ("clus", "trip", "mode"))
    cl, half, flat = force_third.shape
    points, modes, _ = eigenvectors.shape
    slot = send_rows.shape[1] // n_trip
    rounds = plan(flat)
    count = len(rounds)
    rp = up(half, 16)
    ep = up(modes + 1, 16)
    share = sum(width for _, _, width, _ in rounds)
    npad = share * WORKERS
    elanes = up(2 * modes, LANES)
    n_peers = n_clus * n_trip - 1
    vmem = pl.BlockSpec(memory_space=pltpu.VMEM)
    smem = pl.BlockSpec(memory_space=pltpu.SMEM)
    out = jax.ShapeDtypeStruct(boundary.shape, f32)
    dma = pltpu.SemaphoreType.DMA
    return tuple(
        pl.pallas_call(
            functools.partial(kernel, (n_clus, n_trip, n_mode, modes, half, rp, cl, slot, rounds)),
            out_shape=(out, out),
            in_specs=[vmem, vmem, vmem, vmem, vmem, smem, smem, smem, smem, vmem, vmem],
            out_specs=(vmem, vmem),
            scratch_shapes=[
                pltpu.VMEM((cl * rp, npad), bf16),
                pltpu.VMEM((n_mode, n_clus, cl * rp, share), bf16),
                pltpu.VMEM((4, n_mode, 2 * rp, share), bf16),
                pltpu.VMEM((2 * rp, npad), bf16),
                pltpu.VMEM((2 * rp, npad), bf16),
                pltpu.VMEM((2 * n_clus, 8, LANES), f32),
                pltpu.VMEM((4, SUB, LANES), f32),
                pltpu.VMEM((2, LANES, LANES), bf16),
                pltpu.VMEM((2 * rp, 2 * n_mode * rp), bf16),
                pltpu.VMEM((2 * ep, 2 * ep), bf16),
                pltpu.VMEM((points, rp, elanes), f32),
                pltpu.VMEM((8, LANES), f32),
                pltpu.VMEM((n_trip, 8, LANES), f32),
                pltpu.VMEM((n_trip, 3, rp, elanes), bf16),
                pltpu.VMEM((n_trip, 3, rp, elanes), bf16),
                pltpu.VMEM((3, rp, elanes), bf16),
                pltpu.VMEM((3, rp, elanes), bf16),
                pltpu.VMEM((3, 2, ep, LANES), f32),
                pltpu.VMEM((2 * rp, npad), f32),
                pltpu.VMEM((ep * rp, LANES), f32),
                pltpu.VMEM((ep * rp, LANES), f32),
                pltpu.VMEM((8 + rp, LANES), f32),
                pltpu.VMEM((rp, ep, LANES), f32),
                pltpu.VMEM((rp * 8, LANES), f32),
                pltpu.VMEM((rp * 8, LANES), f32),
                pltpu.VMEM((8, LANES), f32),
                pltpu.VMEM((n_peers, 8, LANES), f32),
                dma((count, 7)),
                dma((count, n_mode, n_clus)),
                dma((count, 7)),
                dma((count, WORKERS)),
                dma((count,)),
                dma((count,)),
                dma((n_trip,)),
                dma((n_trip,)),
                dma((2 * n_clus,)),
                dma((2 * n_clus,)),
                dma((n_trip,)),
                dma((n_trip,)),
                dma,
                dma,
                dma((n_peers,)),
                dma((n_peers,)),
            ],
            compiler_params=pltpu.CompilerParams(
                collective_id=0, has_side_effects=True, vmem_limit_bytes=48 * 1024 * 1024
            ),
        )(
            force_third,
            phase_angle,
            eigenvectors,
            frequencies,
            deviation,
            send_rows,
            trip_table,
            irreducible,
            multiplicity,
            drive_term,
            boundary,
        )
    )


def solution(mesh):
    return jax.shard_map(
        body,
        mesh=mesh,
        in_specs=(
            P("clus", "mode", None),
            P("clus", "trip"),
            P("trip", None, None),
            P("trip", None),
            P("trip", None),
            P("trip", None),
            P("trip", None),
            P("trip"),
            P("trip"),
            P("trip", "mode"),
            P("trip", "mode"),
        ),
        out_specs=(P("trip", "mode"), P("trip", "mode")),
        check_vma=False,
    )
```

```python
import functools

import jax
import jax.numpy as jnp
from jax import lax
from jax.experimental import pallas as pl
from jax.experimental.pallas import tpu as pltpu
from jax.sharding import PartitionSpec as P

smearing = 0.3
MESH = pl.DeviceIdType.MESH
LANES = 128
SUB = 16
WORKERS = 8
NEAR = 0
VMEM_BYTES = 66 * 1000 * 1000
f32 = jnp.float32
bf16 = jnp.bfloat16


def up(value, step):
    return -(-value // step) * step


def pick(index, options):
    chosen = options[0]
    for position in range(1, len(options)):
        chosen = jnp.where(index == position, options[position], chosen)
    return chosen


def flip(bit, by):
    return bit + by - 2 * bit * by


def plan(flat):
    left = -(-flat // (WORKERS * LANES))
    units = [1] if left > 2 else []
    left -= sum(units)
    while left > 0:
        units.append(min(2, left))
        left -= units[-1]
    rounds, base, col = [], 0, 0
    for index, unit in enumerate(units):
        rounds.append((index % 2, base, unit * LANES, col, index < NEAR))
        base += unit * LANES * WORKERS
        col += unit * LANES
    return rounds


def kernel(
    dims,
    force_ref,
    eig_ref,
    angle_hbm,
    freq_hbm,
    occ_hbm,
    send_rows_hbm,
    table_hbm,
    irr_hbm,
    mult_hbm,
    drive_hbm,
    bound_hbm,
    out_ref,
    angle_ref,
    freq_ref,
    occ_ref,
    send_rows_ref,
    table_ref,
    irr_ref,
    mult_ref,
    drive_ref,
    bound_ref,
    lin,
    elin,
    own,
    fbuf,
    gout,
    gin,
    gsib,
    tails,
    lset,
    wphase,
    wz,
    left,
    ehalf,
    asked,
    wanted,
    outgoing,
    arrived,
    mine,
    other,
    ebuf,
    zbuf,
    tre,
    tim,
    w0buf,
    gauss,
    ratebuf,
    coupbuf,
    msg,
    inbox,
    f_send,
    f_recv,
    g_send,
    g_recv,
    s_send,
    s_recv,
    t_send,
    t_recv,
    c_send,
    c_recv,
    e_send,
    e_recv,
    p_send,
    p_recv,
    m_send,
    m_recv,
    l_sem,
):
    n_clus, n_trip, n_mode, modes, half, rp, cl, slot, rounds = dims
    ep = up(modes + 1, 16)
    flat = lin.shape[2]
    wide = own.shape[1]
    c = lax.axis_index("clus")
    t = lax.axis_index("trip")
    m = lax.axis_index("mode")
    k = lax.rem(t, 2)
    tz = t + 1 - 2 * k
    bits = (lax.rem(c, 2), c // 2)
    step = (1 - 2 * bits[0], 2 - 4 * bits[1])
    sib = (c, t, 1 - m)
    first = m == 0

    fetch_eig = pltpu.make_async_copy(eig_ref.at[pl.ds(m * half, half)], elin, l_sem.at[0])
    fetch_force = pltpu.make_async_copy(force_ref, lin, l_sem.at[1])
    fetches = []
    small = (
        (table_hbm, table_ref),
        (angle_hbm, angle_ref),
        (freq_hbm, freq_ref),
        (occ_hbm, occ_ref),
        (send_rows_hbm, send_rows_ref),
        (irr_hbm, irr_ref),
        (mult_hbm, mult_ref),
        (drive_hbm, drive_ref),
        (bound_hbm, bound_ref),
    )
    for index, (src, dst) in enumerate(small):
        copy = pltpu.make_async_copy(src, dst, l_sem.at[2 + index])
        copy.start()
        fetches.append(copy)
    fetch_force.start()
    fetch_eig.start()

    peers = []
    for dt in range(n_trip):
        for dc in range(n_clus):
            if dt or dc:
                peers.append((dt, dc))

    def peer_id(dt, dc):
        return (lax.rem(c + dc, n_clus), lax.rem(t + dt, n_trip), m)

    def clus_at(axis, du):
        return c + step[axis] if du else c

    across = [sib]
    for axis in range(2):
        for dk in range(2):
            across.append((clus_at(axis, 1), tz if dk else t, 1 - m))
    across.append((c, tz, 1 - m))
    across.append((c + step[0] + step[1], t, 1 - m))

    barrier = pltpu.get_barrier_semaphore()
    for dt, dc in peers:
        pl.semaphore_signal(barrier, inc=1, device_id=peer_id(dt, dc), device_id_type=MESH)
    for device in across:
        pl.semaphore_signal(barrier, inc=1, device_id=device, device_id_type=MESH)

    for copy in fetches:
        copy.wait()
    asked[...] = jnp.zeros_like(asked)
    for j in range(3):
        asked[j : j + 1, :] = jnp.full((1, LANES), table_ref[c, j].astype(f32))

    angles = angle_ref[...].astype(f32)
    here = k * n_clus + c
    tails[here] = jnp.zeros((8, LANES), f32)
    tails[here, 0:cl, 0 : angles.shape[1]] = jnp.cos(angles).astype(bf16).astype(f32)
    tails[here, cl : 2 * cl, 0 : angles.shape[1]] = jnp.sin(angles).astype(bf16).astype(f32)

    points = freq_ref.shape[0]
    ehalf[...] = jnp.zeros_like(ehalf)
    extra = jnp.where(first, freq_ref[...].astype(f32), occ_ref[...].astype(f32))
    for p in range(points):
        ehalf[p, half : half + 1, 0:modes] = extra[p : p + 1]

    def relayout(lo, hi):
        top = min(hi, flat)
        if hi > flat:
            edge = flat // LANES * LANES
            own[:, edge:hi] = jnp.zeros((cl * rp, hi - edge), bf16)
        for a in range(0, half, SUB):
            n = min(SUB, half - a)
            part = lin[a : a + n, :, lo:top]
            if n < SUB:
                part = jnp.concatenate([part, jnp.zeros((SUB - n, cl, top - lo), bf16)], axis=0)
            own[a * cl : (a + SUB) * cl, lo:top] = part.reshape(SUB * cl, top - lo)

    def components():
        ehalf[:, 0:half, 0 : 2 * modes] = jnp.transpose(elin[...].astype(f32), (1, 0, 2))

    def prepare(e):
        relayout(rounds[e][1], rounds[e][1] + WORKERS * rounds[e][2])

    fetch_force.wait()
    prepare(0)
    pl.semaphore_wait(barrier, len(peers) + len(across))

    started = []

    def remote(src, dst, send_sem, recv_sem, device):
        return pltpu.make_async_remote_copy(
            src_ref=src,
            dst_ref=dst,
            send_sem=send_sem,
            recv_sem=recv_sem,
            device_id=device,
            device_id_type=MESH,
        )

    def send(src, dst, send_sem, recv_sem, device):
        copy = remote(src, dst, send_sem, recv_sem, device)
        copy.start()
        started.append(copy)

    asks = []
    for dt in range(1, n_trip):
        copy = remote(asked, wanted.at[dt], t_send.at[dt], t_recv.at[dt], (c, lax.rem(t + dt, n_trip), m))
        copy.start()
        asks.append(copy)

    cube = []
    cube_clus = [c, c + step[0], c + step[1], c + step[0] + step[1]]
    for dk in range(2):
        for dc in range(n_clus):
            if dk or dc:
                cube.append((dk, dc))
    for index, (dk, dc) in enumerate(cube):
        send(
            tails.at[here],
            tails.at[here],
            c_send.at[index],
            c_recv.at[here],
            (cube_clus[dc], tz if dk else t, m),
        )

    def worker(ub, kk, mm):
        return (ub * 2 + kk) * 2 + mm

    def columns(e, w):
        _, base, width, _, _ = rounds[e]
        return pl.ds(pl.multiple_of(base + w * width, LANES), width)

    def local(e):
        return pl.ds(rounds[e][3], rounds[e][2])

    def lines(e):
        axis = rounds[e][0]
        cu, cv = clus_at(axis, 1), clus_at(1 - axis, 1)
        return bits[axis], cu, cv, c + step[0] + step[1]

    def direct(e):
        ub, cu, cv, cd = lines(e)
        dst = fbuf.at[m, c, :, local(e)]
        recv = f_recv.at[e, m, c]
        for index, mm in enumerate((m, 1 - m)):
            send(own.at[:, columns(e, worker(1 - ub, k, mm))], dst, f_send.at[e, index], recv, (cu, t, mm))
            send(own.at[:, columns(e, worker(ub, k, mm))], dst, f_send.at[e, 2 + index], recv, (cv, t, mm))
        if rounds[e][4]:
            for index, mm in enumerate((m, 1 - m)):
                send(own.at[:, columns(e, worker(1 - ub, k, mm))], dst, f_send.at[e, 5 + index], recv, (cd, t, mm))
        send(own.at[:, columns(e, worker(ub, k, 1 - m))], dst, f_send.at[e, 4], recv, sib)

    def got(e, g, cc):
        ref = fbuf.at[g, cc, :, local(e)]
        remote(ref, ref, f_send.at[e, 0], f_recv.at[e, g, cc], sib).wait_recv()

    def forward(e):
        if rounds[e][4]:
            return
        _, cu, cv, _ = lines(e)
        for g in range(n_mode):
            got(e, g, cu)
            ref = fbuf.at[g, cu, :, local(e)]
            send(ref, ref, f_send.at[e, 5 + g], f_recv.at[e, g, cu], (cv, t, m))

    def phased(e):
        axis = rounds[e][0]
        ub, cu, cv, cd = lines(e)
        me = worker(ub, k, m)
        fbuf[m, c, :, local(e)] = own[:, columns(e, me)]
        got(e, 1 - m, c)
        for g in range(n_mode):
            if rounds[e][4]:
                got(e, g, cu)
            got(e, g, cv)
            got(e, g, cd)
        weights = wphase[axis]
        for g in range(n_mode):
            for a0 in range(0, rp, SUB):
                parts = [fbuf[g, cc, a0 * cl : (a0 + SUB) * cl, local(e)] for cc in range(n_clus)]
                out = jnp.dot(weights, jnp.concatenate(parts, axis=0), preferred_element_type=f32).astype(bf16)
                for q in range(4):
                    for i in range(2):
                        row = (q * 2 + i) * SUB
                        gout[q, g, i * rp + a0 : i * rp + a0 + SUB, local(e)] = out[row : row + SUB]
        dst = gin.at[:, columns(e, me)]
        recv = g_recv.at[e, me]
        index = 0
        for du, dk in ((1, 1), (0, 1), (1, 0)):
            for g in range(n_mode):
                device = (clus_at(axis, du), tz if dk else t, g)
                send(gout.at[du * 2 + dk, g, :, local(e)], dst, g_send.at[e, index], recv, device)
                index += 1
        send(gout.at[0, 1 - m, :, local(e)], dst, g_send.at[e, index], recv, sib)
        gin[:, columns(e, me)] = gout[0, m, :, local(e)]

    def gather(e):
        axis, base, width, _, _ = rounds[e]
        ub = bits[axis]
        for du in range(2):
            for dk in range(2):
                for dm in range(2):
                    if du or dk or dm:
                        w = worker(flip(ub, du), flip(k, dk), flip(m, dm))
                        ref = gin.at[:, columns(e, w)]
                        remote(ref, ref, g_send.at[e, 0], g_recv.at[e, w], sib).wait_recv()
        span = pl.ds(base, WORKERS * width)
        send(gin.at[:, span], gsib.at[:, span], s_send.at[e], s_recv.at[e], sib)

    def answer(dt, wishes):
        target = lax.rem(t - dt + n_trip, n_trip)
        for j in range(3):
            wish = wishes[j : j + 1, 0:1]
            block = jnp.zeros(ehalf.shape[1:], f32)
            for p in range(slot):
                row = send_rows_ref[0, target * slot + p]
                name = (t * slot + p).astype(f32)
                block = jnp.where(wish == name, ehalf[row], block)
            outgoing[dt, j] = block.astype(bf16)

    eig_copies = []

    def answers():
        for dt in range(1, n_trip):
            asks[dt - 1].wait()
            answer(dt, wanted[dt])
        for dt in range(1, n_trip):
            copy = remote(
                outgoing.at[dt],
                arrived.at[dt],
                e_send.at[dt],
                e_recv.at[dt],
                (c, lax.rem(t - dt + n_trip, n_trip), m),
            )
            copy.start()
            eig_copies.append(copy)
        answer(0, asked[...])
        arrived[0] = outgoing[0]

    lane = lax.broadcasted_iota(jnp.int32, (1, LANES), 1)

    def phase_weights():
        for dk, dc in cube:
            there = flip(k, dk) * n_clus + cube_clus[dc]
            ref = tails.at[there]
            remote(ref, ref, c_send.at[0], c_recv.at[there], sib).wait_recv()
        stack = jnp.concatenate([tails[i] for i in range(2 * n_clus)], axis=0)
        stack = jnp.concatenate([stack, jnp.zeros((LANES - stack.shape[0], LANES), f32)], axis=0)
        turned = jnp.transpose(stack)[:SUB].astype(bf16)
        row = lax.broadcasted_iota(jnp.int32, (LANES, LANES), 0)
        col = lax.broadcasted_iota(jnp.int32, (LANES, LANES), 1)
        source = (col // (cl * SUB)) * 8 + lax.rem(col, cl)
        for kk in range(2):
            for i in range(2):
                spread = jnp.where(row == source + (kk * n_clus * 8 + i * cl), 1.0, 0.0).astype(bf16)
                lset[kk * 2 + i] = jnp.dot(turned, spread, preferred_element_type=f32)
        same = lax.broadcasted_iota(jnp.int32, (SUB, LANES), 0) == lax.rem(
            lax.broadcasted_iota(jnp.int32, (SUB, LANES), 1) // cl, SUB
        )
        for axis in range(2):
            for du in range(2):
                for dk in range(2):
                    for i in range(2):
                        values = lset[flip(k, dk) * 2 + i, pl.ds(clus_at(axis, du), 1), :]
                        at = ((du * 2 + dk) * 2 + i) * SUB
                        wphase[axis, at : at + SUB, :] = jnp.where(same, values, 0.0).astype(bf16)

    pair = remote(mine, other, p_send, p_recv, sib)

    def members():
        for copy in eig_copies:
            copy.wait()
        for j in range(3):
            source = table_ref[c, j] // slot
            mine[j] = arrived[lax.rem(source - t + n_trip, n_trip), j]
        pair.start()

    fill = jnp.zeros((LANES - 2 * rp, LANES), f32)
    state = {}

    def half_rows(mat, which):
        return pick(which, [mat[h * half : h * half + rp] for h in range(n_mode)])

    def column(row):
        return jnp.transpose(jnp.broadcast_to(row, (LANES, LANES)))

    def vectors():
        pair.wait()
        ebuf[...] = jnp.zeros_like(ebuf)
        freqs, occs = [], []
        for j in range(3):
            a = mine[j].astype(f32)
            b = other[j].astype(f32)
            parts = jnp.where(first, a, b), jnp.where(first, b, a)
            for g in range(n_mode):
                at = g * rp if j == 0 else g * half
                ebuf[j, 0, at : at + half, 0:modes] = parts[g][:half, 0:modes]
                ebuf[j, 1, at : at + half, 0:modes] = parts[g][:half, modes : 2 * modes]
            w0buf[2 * j : 2 * j + 1, 0:LANES] = parts[0][half : half + 1, 0:LANES]
            w0buf[2 * j + 1 : 2 * j + 2, 0:LANES] = parts[1][half : half + 1, 0:LANES]
            freqs.append(w0buf[2 * j : 2 * j + 1, :])
            occs.append(w0buf[2 * j + 1 : 2 * j + 2, :])
        f0, f1, f2 = freqs
        _, d1, d2 = occs
        for place, g in enumerate((m, 1 - m)):
            re0 = ebuf[0, 0, pl.ds(pl.multiple_of(g * rp, 16), rp), :]
            im0 = ebuf[0, 1, pl.ds(pl.multiple_of(g * rp, 16), rp), :]
            real = half_rows(jnp.transpose(jnp.concatenate([re0, -im0, fill], axis=0)), m)
            imag = half_rows(jnp.transpose(jnp.concatenate([im0, re0, fill], axis=0)), m)
            turned = jnp.concatenate([real, imag], axis=0)[:, : 2 * rp].astype(bf16)
            wz[:, place * 2 * rp : (place + 1) * 2 * rp] = turned
        re1, im1 = ebuf[1, 0], ebuf[1, 1]
        re2, im2 = ebuf[2, 0], ebuf[2, 1]
        state["e2a"] = jnp.concatenate([re2, im2], axis=1)[:modes].astype(bf16)
        state["e2b"] = jnp.concatenate([-im2, re2], axis=1)[:modes].astype(bf16)
        tall = jnp.zeros((LANES - ep, LANES), f32)
        e1re_t = jnp.transpose(jnp.concatenate([re1, tall], axis=0))[:ep, :ep]
        e1im_t = jnp.transpose(jnp.concatenate([im1, tall], axis=0))[:ep, :ep]
        left[:, :ep] = jnp.concatenate([e1re_t, e1im_t], axis=0).astype(bf16)
        left[:, ep:] = jnp.concatenate([-e1im_t, e1re_t], axis=0).astype(bf16)
        row_id = lax.broadcasted_iota(jnp.int32, (ep, LANES), 0)
        state["w0row"] = f0
        state["w0"] = half_rows(column(f0), m)
        w1 = jnp.where(row_id < modes, column(f1)[:ep], 1.0)
        w2 = jnp.where(lane < modes, f2, 1.0)
        state["occ"] = jnp.where(row_id < modes, column(d1)[:ep], 0.0) + jnp.where(lane < modes, d2, 0.0)
        state["inverse"] = 1.0 / (w1 * w2)
        state["lower"] = w1 + w2
        state["upper"] = w1 - w2
        tre[modes * rp :, :] = jnp.zeros(((ep - modes) * rp, LANES), f32)
        tim[modes * rp :, :] = jnp.zeros(((ep - modes) * rp, LANES), f32)
        w0buf[8:, :] = state["w0"]

    scaled = 0.5 / (smearing * smearing)

    def gaussians(lo, hi):
        lower, upper, inverse = state["lower"], state["upper"], state["inverse"]

        def one(s, carry):
            w0 = w0buf[pl.ds(8 + s, 1), :]
            decays = w0 - lower
            merges = w0 + upper
            both = jnp.exp(-scaled * (decays * decays)) + jnp.exp(-scaled * (merges * merges))
            gauss[s] = both * inverse
            return carry

        lax.fori_loop(lo, hi, one, 0)

    def contract(e):
        _, base, width, _, _ = rounds[e]
        lo, hi = base, base + WORKERS * width
        span = pl.ds(lo, hi - lo)
        ref = gsib.at[:, span]
        remote(ref, ref, s_send.at[e], s_recv.at[e], sib).wait_recv()
        for at in range(lo, hi, 512):
            cols = slice(at, at + 512)
            both = jnp.concatenate([gin[:, cols], gsib[:, cols]], axis=0)
            zbuf[:, cols] = jnp.dot(wz[...], both, preferred_element_type=f32)
        for b in range(modes):
            if not lo < (b + 1) * modes <= hi:
                continue
            part = zbuf[:, b * modes : (b + 1) * modes].astype(bf16)
            out = jnp.dot(part[:rp], state["e2a"], preferred_element_type=f32) + jnp.dot(
                part[rp:], state["e2b"], preferred_element_type=f32
            )
            tre[b * rp : (b + 1) * rp, :] = out[:, :LANES]
            tim[b * rp : (b + 1) * rp, :] = out[:, LANES:]

    total = len(rounds)

    direct(0)
    for e in range(1, total):
        prepare(e)
        if e < 2:
            direct(e)
    fetch_eig.wait()
    components()
    forward(0)
    if total > 2:
        direct(2)
    answers()
    phase_weights()
    for e in range(total):
        if e + 1 < total:
            forward(e + 1)
        if e + 3 < total:
            direct(e + 3)
        phased(e)
        if e == 1:
            members()
        if e == 2:
            gather(0)
            vectors()
        if e >= 3:
            gather(e - 2)
            contract(e - 3)
            gaussians((e - 3) * rp // 2, (e - 2) * rp // 2)
    gaussians(max(total - 3, 0) * rp // 2, rp)
    for e in range(max(total - 3, 0), total):
        if e + 1 < total:
            gather(e + 1)
        contract(e)

    occ = state["occ"]

    def one_pair(s0):
        def rows(ref):
            return jnp.concatenate(
                [ref[pl.ds(s0 + i, ep, stride=rp), :] for i in range(2)], axis=1
            ).astype(bf16)

        both = jnp.concatenate([rows(tre), rows(tim)], axis=0)
        amp = jnp.dot(left[...], both, preferred_element_type=f32)
        square = amp * amp
        square = square[:ep] + square[ep:]
        for i in range(2):
            value = square[:, i * LANES : (i + 1) * LANES] * gauss[s0 + i]
            at = pl.ds(pl.multiple_of((s0 + i) * 8, 8), 8)
            ratebuf[at, :] = jnp.sum(value.reshape(ep // 8, 8, LANES), axis=0)
            coupbuf[at, :] = jnp.sum((value * occ).reshape(ep // 8, 8, LANES), axis=0)

    group = 4

    def modes_step(p, carry):
        for i in range(group):
            one_pair((p * group + i) * 2)
        return carry

    lax.fori_loop(0, rp // (2 * group), modes_step, 0)

    def folded(ref):
        total = ref[pl.ds(0, rp, stride=8), :]
        for i in range(1, 8):
            total = total + ref[pl.ds(i, rp, stride=8), :]
        return jnp.sum(jnp.transpose(total), axis=0, keepdims=True)[:, :half]

    factor = mult_ref[c].astype(f32)
    f0 = state["w0row"]
    w0_row = pick(m, [f0[:, h * half : (h + 1) * half] for h in range(n_mode)])
    rate = folded(ratebuf) / w0_row * factor
    coup = folded(coupbuf) / w0_row * factor
    msg[...] = jnp.zeros_like(msg)
    msg[0:1, 0:half] = rate
    msg[1:2, 0:half] = coup
    msg[2:3, :] = jnp.full((1, LANES), irr_ref[c].astype(f32))

    copies = []
    for index, (dt, dc) in enumerate(peers):
        copy = remote(msg, inbox.at[index], m_send.at[index], m_recv.at[index], peer_id(dt, dc))
        copy.start()
        copies.append(copy)
    for copy in started:
        copy.wait_send()
    for copy in copies:
        copy.wait()

    nq = out_ref.shape[1]
    for q in range(nq):
        name = (t * nq + q).astype(f32)

        def kept(tile):
            return jnp.where(tile[2:3, :half] == name, tile[0:2, :half], 0.0)

        total = kept(msg[...])
        if len(peers) <= 16:
            for index in range(len(peers)):
                total = total + kept(inbox[index])
        else:
            total = lax.fori_loop(0, len(peers), lambda i, acc: acc + kept(inbox[i]), total)
        gamma = total[0:1] + bound_ref[q : q + 1, :]
        out_ref[0, q : q + 1, :] = gamma
        out_ref[1, q : q + 1, :] = (drive_ref[q : q + 1, :] + total[1:2]) / gamma


def body(
    force_third,
    phase_angle,
    eigenvectors,
    frequencies,
    deviation,
    send_rows,
    trip_table,
    irreducible,
    multiplicity,
    drive_term,
    boundary,
):
    n_clus, n_trip, n_mode = (lax.axis_size(name) for name in ("clus", "trip", "mode"))
    cl, half, flat = force_third.shape
    points, modes, _ = eigenvectors.shape
    force_third = jnp.transpose(force_third, (1, 0, 2))
    eigenvectors = jnp.transpose(eigenvectors, (1, 0, 2))
    slot = send_rows.shape[1] // n_trip
    rounds = plan(flat)
    count = len(rounds)
    rp = up(half, 16)
    ep = up(modes + 1, 16)
    share = sum(width for _, _, width, _, _ in rounds)
    npad = share * WORKERS
    elanes = up(2 * modes, LANES)
    n_peers = n_clus * n_trip - 1
    vmem = pl.BlockSpec(memory_space=pltpu.VMEM)
    small = (
        (phase_angle, pltpu.VMEM),
        (frequencies, pltpu.VMEM),
        (deviation, pltpu.VMEM),
        (send_rows, pltpu.SMEM),
        (trip_table, pltpu.SMEM),
        (irreducible, pltpu.SMEM),
        (multiplicity, pltpu.SMEM),
        (drive_term, pltpu.VMEM),
        (boundary, pltpu.VMEM),
    )
    anywhere = pl.BlockSpec(memory_space=pl.ANY)
    out = jax.ShapeDtypeStruct((2,) + boundary.shape, f32)
    dma = pltpu.SemaphoreType.DMA
    packed = (
        pl.pallas_call(
            functools.partial(kernel, (n_clus, n_trip, n_mode, modes, half, rp, cl, slot, rounds)),
            out_shape=out,
            in_specs=[anywhere] * (2 + len(small)),
            out_specs=vmem,
            scratch_shapes=[space(value.shape, value.dtype) for value, space in small]
            + [
                pltpu.VMEM((half, cl, flat), bf16),
                pltpu.VMEM((half, points, 2 * modes), bf16),
                pltpu.VMEM((cl * rp, npad), bf16),
                pltpu.VMEM((n_mode, n_clus, cl * rp, share), bf16),
                pltpu.VMEM((4, n_mode, 2 * rp, share), bf16),
                pltpu.VMEM((2 * rp, npad), bf16),
                pltpu.VMEM((2 * rp, npad), bf16),
                pltpu.VMEM((2 * n_clus, 8, LANES), f32),
                pltpu.VMEM((4, SUB, LANES), f32),
                pltpu.VMEM((2, LANES, LANES), bf16),
                pltpu.VMEM((2 * rp, 2 * n_mode * rp), bf16),
                pltpu.VMEM((2 * ep, 2 * ep), bf16),
                pltpu.VMEM((points, rp, elanes), f32),
                pltpu.VMEM((8, LANES), f32),
                pltpu.VMEM((n_trip, 8, LANES), f32),
                pltpu.VMEM((n_trip, 3, rp, elanes), bf16),
                pltpu.VMEM((n_trip, 3, rp, elanes), bf16),
                pltpu.VMEM((3, rp, elanes), bf16),
                pltpu.VMEM((3, rp, elanes), bf16),
                pltpu.VMEM((3, 2, ep, LANES), f32),
                pltpu.VMEM((2 * rp, npad), f32),
                pltpu.VMEM((ep * rp, LANES), f32),
                pltpu.VMEM((ep * rp, LANES), f32),
                pltpu.VMEM((8 + rp, LANES), f32),
                pltpu.VMEM((rp, ep, LANES), f32),
                pltpu.VMEM((rp * 8, LANES), f32),
                pltpu.VMEM((rp * 8, LANES), f32),
                pltpu.VMEM((8, LANES), f32),
                pltpu.VMEM((n_peers, 8, LANES), f32),
                dma((count, 7)),
                dma((count, n_mode, n_clus)),
                dma((count, 7)),
                dma((count, WORKERS)),
                dma((count,)),
                dma((count,)),
                dma((n_trip,)),
                dma((n_trip,)),
                dma((2 * n_clus,)),
                dma((2 * n_clus,)),
                dma((n_trip,)),
                dma((n_trip,)),
                dma,
                dma,
                dma((n_peers,)),
                dma((n_peers,)),
                dma((2 + len(small),)),
            ],
            compiler_params=pltpu.CompilerParams(
                collective_id=0, has_side_effects=True, vmem_limit_bytes=VMEM_BYTES
            ),
        )(force_third, eigenvectors, *(value for value, _ in small))
    )
    return packed[0], packed[1]


def solution(mesh):
    return jax.shard_map(
        body,
        mesh=mesh,
        in_specs=(
            P("clus", "mode", None),
            P("clus", "trip"),
            P("trip", None, None),
            P("trip", None),
            P("trip", None),
            P("trip", None),
            P("trip", None),
            P("trip"),
            P("trip"),
            P("trip", "mode"),
            P("trip", "mode"),
        ),
        out_specs=(P("trip", "mode"), P("trip", "mode")),
        check_vma=False,
    )
```
